32 devices in a mesh: groups: 2 (over y), expert: 8 (over z, x), tensor: 2 (over core).
Axes of the slice: x: 2, y: 2, z: 4, core: 2. Of those that a mesh axis runs over, the one named last changes fastest.
Arguments:
- conv_input: bfloat16 [32, 8192], P(('groups', 'expert'), 'tensor'), parts along dimension 0, may hold values from -6 to 6
- gate_input: bfloat16 [32, 8192], P(('groups', 'expert'), 'tensor'), parts along dimension 0, may hold values from -6 to 6
- step_input: bfloat16 [32, 8192], P(('groups', 'expert'), 'tensor'), parts along dimension 0, may hold values from -6 to 6
- b_proj: float32 [32, 16], P(('groups', 'expert')), parts along dimension 0, may hold values from -6 to 6
- c_proj: float32 [32, 16], P(('groups', 'expert')), parts along dimension 0, may hold values from -6 to 6
- slot_ids: int32 [32], P(('groups', 'expert')), parts along dimension 0, may hold values from 0 to 15, as said below
- state_pool: bfloat16 [32, 16, 8192], P(('groups', 'expert'), None, 'tensor'), parts along dimension 0, may hold values from -6 to 6
- conv_pool: bfloat16 [32, 3, 8192], P(('groups', 'expert'), None, 'tensor'), parts along dimension 0, may hold values from -6 to 6
- conv_weight: float32 [4, 8192], P(None, 'tensor'), may hold values from -4 to 4
- conv_bias: float32 [8192], P('tensor'), may hold values from -4 to 4
- step_bias: float32 [8192], P('tensor'), may hold values from -4 to 0
- a_log: float32 [16, 8192], P(None, 'tensor'), may hold values from -1 to 2.5
- d_skip: float32 [8192], P('tensor'), may hold values from 0.5 to 1.5
- out_weight: bfloat16 [8192, 4096], P('tensor', 'expert'), may hold values from -0.0625 to 0.0625
- residual: bfloat16 [32, 4096], P(('groups', 'expert')), parts along dimension 0, may hold values from -6 to 6
- norm_gain: float32 [4096], replicated, may hold values from 0.5 to 1.5
- expert_ids: int32 [32, 2], P(('groups', 'expert')), parts along dimension 0, may hold values from 0 to 2, all different within a row
- expert_probs: bfloat16 [32, 2], P(('groups', 'expert')), parts along dimension 0, may hold values from 0.19921875 to 1
- gate_weight: bfloat16 [36864, 4096], P(('expert', 'tensor')), may hold values from -0.09375 to 0.09375
- up_weight: bfloat16 [36864, 4096], P(('expert', 'tensor')), may hold values from -0.09375 to 0.09375
- down_weight: bfloat16 [36864, 4096], P(('expert', 'tensor')), may hold values from -0.0546875 to 0.0546875
Outputs:
- layer_out: bfloat16 [32, 4096], P(('groups', 'expert')), parts along dimension 0
- new_state: bfloat16 [32, 16, 8192], P(('groups', 'expert'), None, 'tensor'), parts along dimension 0
The draws below stay inside these ranges and needn't reach their ends.
There are 2 independent parts, one for each index of `groups`. The reference program is written for one: setup_inputs(seed, part) draws one part's arguments, and reference() takes and returns one part's arrays. A program takes and returns all parts, laid end to end along the dimension named above; an argument that names none is the same for every part. Nothing has to cross between parts.
Inputs may be any that keep to these rules, and one draw needn't show every extreme that they name: `slot_ids`: the rows of one index of expert (rows d*2 to (d+1)*2 - 1) use distinct slots among d*2 to (d+1)*2 - 1. `expert_ids`: each row names two different experts.
All inputs are finite; a program needn't handle non-finite values.
Results may differ from the reference program's by a relative error of at most 0.0063.
Values may be sent and summed in bfloat16 or wider, within the bound.
A program may use at most 128 MiB of HBM per device.

```python
import jax
import jax.numpy as jnp
from jax import lax

D = 4096
CH = 8192
NS = 16
KC = 4
EXPERTS = 3
FF = 12288
ROWS_DEV = 2
POOL_DEV = 2
ROWS = 16
SLOTS = 16


def draw_slot_ids(key, part):
    devices = ROWS // ROWS_DEV
    scores = jax.random.randint(key, (devices, POOL_DEV), 0, 1 << 20)
    scores = scores * POOL_DEV + jnp.arange(POOL_DEV, dtype=jnp.int32)[None, :]
    ranking = jnp.argsort(scores, axis=1).astype(jnp.int32)
    chosen = ranking[:, :ROWS_DEV] + (jnp.arange(devices, dtype=jnp.int32) * POOL_DEV)[:, None]
    return chosen.reshape(ROWS).astype(jnp.int32)


def steps_of(key, shape, pieces, low, largest):
    def one(position, parts):
        draws = jax.random.uniform(jax.random.fold_in(jax.random.fold_in(key, 6), position), (parts,), jnp.float32, low / len(pieces), largest / len(pieces))
        return jnp.repeat(jnp.exp(draws), shape[position] // parts).reshape((-1,) + (1,) * (len(shape) - position - 1))

    gain = one(*pieces[0])
    for cut in pieces[1:]:
        gain = gain * one(*cut)
    return gain


def distinct(own_key, rows, number_of, top, lift):
    order = jax.random.permutation(jax.random.fold_in(own_key, 1), number_of)
    favour = order
    for power in range(3):
        favour = favour * favour // number_of
    favour = favour * lift // number_of
    tickets = jax.random.randint(jax.random.fold_in(own_key, 2), (rows, number_of), 0, 4096) + favour
    sure = jax.random.permutation(jax.random.fold_in(own_key, 3), rows)[jnp.arange(number_of) % rows]
    tickets = jnp.where(jnp.arange(rows)[:, None] == sure[None, :], 1 << 14, tickets)
    merit = tickets * number_of + jnp.arange(number_of)
    return lax.top_k(merit.astype(jnp.int32), top)[1].astype(jnp.int32)


def normal_values(own_key, shape, deviation, bound, shards=(), kind=jnp.bfloat16):
    factor_of = steps_of(own_key, shape, shards, -0.22, 0.18) if shards else 1.0
    values = jax.random.normal(own_key, shape, jnp.float32) * deviation * factor_of
    return jnp.minimum(jnp.maximum(values, -bound), bound).astype(kind)


def setup_inputs(seed: int = 0, part: int = 0) -> dict:
    streams_of = jax.random.split(jax.random.key(seed), 22)
    part_keys = jax.random.split(jax.random.fold_in(streams_of[21], part), 22)
    return {
        "conv_input": normal_values(part_keys[0], (ROWS, CH), 1.0, 6.0, ((0, 8), (1, 2))),
        "gate_input": normal_values(part_keys[1], (ROWS, CH), 1.0, 6.0, ((0, 8), (1, 2))),
        "step_input": normal_values(part_keys[2], (ROWS, CH), 1.0, 6.0, ((0, 8), (1, 2))),
        "b_proj": normal_values(part_keys[3], (ROWS, NS), 1.0, 6.0, ((0, 8),), jnp.float32),
        "c_proj": normal_values(part_keys[4], (ROWS, NS), 0.5, 6.0, ((0, 8),), jnp.float32),
        "slot_ids": draw_slot_ids(jax.random.fold_in(jax.random.fold_in(streams_of[21], part), 71), part),
        "state_pool": normal_values(part_keys[6], (SLOTS, NS, CH), 1.0, 6.0, ((0, 8), (2, 2))),
        "conv_pool": normal_values(part_keys[7], (SLOTS, KC - 1, CH), 1.0, 6.0, ((0, 8), (2, 2))),
        "conv_weight": normal_values(streams_of[8], (KC, CH), 0.5, 4.0, ((1, 2),), jnp.float32),
        "conv_bias": normal_values(streams_of[9], (CH,), 0.5, 4.0, ((0, 2),), jnp.float32),
        "step_bias": jnp.clip(-4.0 + 4.0 * jax.random.uniform(streams_of[10], (CH,), jnp.float32) ** steps_of(streams_of[10], (CH,), ((0, 2),), -0.2, 0.2), -4.0, 0.0),
        "a_log": jnp.clip(-1.0 + 3.5 * jax.random.uniform(streams_of[11], (NS, CH), jnp.float32) ** steps_of(streams_of[11], (NS, CH), ((1, 2),), -0.2, 0.2), -1.0, 2.5),
        "d_skip": jnp.clip(0.5 + 1.0 * jax.random.uniform(streams_of[12], (CH,), jnp.float32) ** steps_of(streams_of[12], (CH,), ((0, 2),), -0.2, 0.2), 0.5, 1.5),
        "out_weight": normal_values(streams_of[13], (CH, D), CH ** -0.5, 0.0625, ((0, 2), (1, 8))),
        "residual": normal_values(part_keys[14], (ROWS, D), 1.0, 6.0, ((0, 8),)),
        "norm_gain": jnp.clip(1.0 + 0.1 * jax.random.normal(streams_of[15], (D,), jnp.float32), 0.5, 1.5),
        "expert_ids": distinct(part_keys[16], ROWS, EXPERTS, 2, 10922),
        "expert_probs": jnp.clip(0.19921875 + 0.80078125 * jax.random.uniform(part_keys[17], (ROWS, 2), jnp.float32) ** steps_of(part_keys[17], (ROWS, 2), ((0, 8),), -0.2, 0.2), 0.19921875, 1.0).astype(jnp.bfloat16),
        "gate_weight": normal_values(streams_of[18], (EXPERTS * FF, D), D ** -0.5, 0.09375, ((0, 16),)),
        "up_weight": normal_values(streams_of[19], (EXPERTS * FF, D), D ** -0.5, 0.09375, ((0, 16),)),
        "down_weight": normal_values(streams_of[20], (EXPERTS * FF, D), FF ** -0.5, 0.0546875, ((0, 16),)),
    }


def mamba_step(states, history, conv_input, gate_input, step_input, b_proj, c_proj, conv_weight, conv_bias, step_bias, a_log, d_skip):
    inputs = conv_input.astype(jnp.float32)
    conv_sum = conv_weight[-1] * inputs + conv_bias
    for lag in range(history.shape[1]):
        conv_sum = conv_sum + conv_weight[lag] * history[:, lag]
    conv_out = jax.nn.silu(conv_sum)
    step_size = jax.nn.softplus(step_input.astype(jnp.float32) + step_bias)
    state_rates = -jnp.exp(a_log)
    decay_rate = jnp.exp(step_size[:, None, :] * state_rates[None])
    state_next = decay_rate * states + (step_size * conv_out)[:, None, :] * b_proj[:, :, None]
    output = lax.optimization_barrier(jnp.sum(c_proj[:, :, None] * state_next, axis=1)) + d_skip * conv_out
    gated_out = (output * jax.nn.silu(gate_input.astype(jnp.float32))).astype(jnp.bfloat16)
    return (state_next, gated_out)

def expert_ffn(rows, gate_part, up_part, down_part):
    dims = (((1,), (1,)), ((), ()))
    gate_act = lax.dot_general(rows, gate_part, dims, preferred_element_type=jnp.float32)
    up_act = lax.dot_general(rows, up_part, dims, preferred_element_type=jnp.float32)
    hidden = (jax.nn.silu(gate_act) * up_act).astype(jnp.bfloat16)
    return jnp.dot(hidden, down_part, preferred_element_type=jnp.float32)

def reference(conv_input, gate_input, step_input, b_proj, c_proj, slot_ids, state_pool, conv_pool, conv_weight, conv_bias, step_bias, a_log, d_skip, out_weight, residual, norm_gain, expert_ids, expert_probs, gate_weight, up_weight, down_weight):
    states = state_pool[slot_ids].astype(jnp.float32)
    history = conv_pool[slot_ids].astype(jnp.float32)
    state_next, gated_out = mamba_step(states, history, conv_input, gate_input, step_input, b_proj, c_proj, conv_weight, conv_bias, step_bias, a_log, d_skip)
    mixed = jnp.dot(gated_out, out_weight, preferred_element_type=jnp.float32).astype(jnp.bfloat16)
    hidden_state = (residual.astype(jnp.float32) + mixed.astype(jnp.float32)).astype(jnp.bfloat16)
    wide = hidden_state.astype(jnp.float32)
    normed = (wide * lax.rsqrt(lax.optimization_barrier(jnp.mean(wide * wide, axis=1, keepdims=True)) + 1e-05) * norm_gain).astype(jnp.bfloat16)
    probs = expert_probs.astype(jnp.float32)

    def one_expert(carry, expert):
        start = (expert * FF).astype(jnp.int32)
        gate_part = lax.dynamic_slice_in_dim(gate_weight, start, FF, 0)
        up_part = lax.dynamic_slice_in_dim(up_weight, start, FF, 0)
        down_part = lax.dynamic_slice_in_dim(down_weight, start, FF, 0)
        result = expert_ffn(normed, gate_part, up_part, down_part)
        weight_row = lax.optimization_barrier(jnp.sum(probs * (expert_ids == expert).astype(jnp.float32), axis=1))
        return (carry + weight_row[:, None] * result, None)
    routed, _ = lax.scan(one_expert, jnp.zeros((normed.shape[0], normed.shape[1]), jnp.float32), jnp.arange(EXPERTS, dtype=jnp.int32))
    layer_out = (hidden_state.astype(jnp.float32) + routed).astype(jnp.bfloat16)
    return (layer_out, state_next.astype(jnp.bfloat16))
```

```python
import functools

import jax
import jax.numpy as jnp
from jax import lax
from jax.experimental import pallas as pl
from jax.experimental.pallas import tpu as pltpu
from jax.sharding import PartitionSpec as P

EXPERTS = 3
LANES = 128
F32 = jnp.float32
BF16 = jnp.bfloat16
TRANS = (((1,), (1,)), ((), ()))
MESH = pl.DeviceIdType.MESH
NJ = 4
SMALL = 16


def unit_block(units):
    for block in (256, 384, 128):
        if units % block == 0:
            return block
    return units


def kernel(
    peers,
    slots,
    *refs,
):
    small_hbm = refs[:SMALL]
    outw_hbm, gate_hbm, up_hbm, down_hbm = refs[SMALL : SMALL + 4]
    out_ref, ns_hbm = refs[SMALL + 4 : SMALL + 6]
    small = refs[SMALL + 6 : 2 * SMALL + 6]
    (
        small_sem,
        outw,
        outw_sem,
        gbuf,
        ubuf,
        dbuf,
        w_sem,
        gsend,
        grecv,
        gs_sem,
        gr_sem,
        rrecv,
        rs_sem,
        rr_sem,
        gat,
        part,
        part_in,
        part_sem,
        mix,
        mrecv,
        ms_sem,
        mr_sem,
        hid,
        normed,
        h3,
        osend,
        orecv,
        os_sem,
        or_sem,
        fin,
        fin_sem,
        nsbuf,
        ns_sem,
    ) = refs[2 * SMALL + 6 :]
    (
        conv_in,
        gate_in,
        step_in,
        b_proj,
        c_proj,
        pool,
        cpool,
        conv_w,
        conv_b,
        step_b,
        a_log,
        d_skip,
        resid,
        gain,
        ids,
        probs,
    ) = small
    e = lax.axis_index("expert")
    t = lax.axis_index("tensor")
    other = 1 - t
    nch, ub, d = gbuf.shape
    rows_dev, chl = conv_in.shape
    rows = rows_dev * peers
    units = nch * ub
    ff = units * peers * 2 // EXPERTS
    cb = outw.shape[1]
    half = d // 2
    nj2 = NJ // 2
    cw = d // NJ

    def peer(k):
        return lax.rem(e + k, peers)

    def each_peer(body):
        def step(k, carry):
            body(peer(k))
            return carry

        lax.fori_loop(1, peers, step, 0)

    barrier = pltpu.get_barrier_semaphore()
    pl.semaphore_signal(
        barrier, inc=1, device_id={"expert": e, "tensor": other}, device_id_type=MESH
    )

    def greet(p):
        pl.semaphore_signal(barrier, inc=1, device_id={"expert": p, "tensor": t}, device_id_type=MESH)
        pl.semaphore_signal(
            barrier, inc=1, device_id={"expert": p, "tensor": other}, device_id_type=MESH
        )

    each_peer(greet)

    loads = [
        pltpu.make_async_copy(src, dst, small_sem.at[i])
        for i, (src, dst) in enumerate(zip(small_hbm, small))
    ]
    for load in loads:
        load.start()
    outw_load = pltpu.make_async_copy(outw_hbm, outw, outw_sem)
    outw_load.start()

    def weight(which, c):
        src, dst = ((gate_hbm, gbuf), (up_hbm, ubuf), (down_hbm, dbuf))[which]
        return pltpu.make_async_copy(
            src.at[pl.ds(pl.multiple_of(c * ub, ub), ub)], dst.at[c], w_sem.at[which, c]
        )

    def start_gate_up(c, carry):
        weight(0, c).start()
        weight(1, c).start()
        return carry

    def start_down(c, carry):
        weight(2, c).start()
        return carry

    lax.fori_loop(0, nch, start_gate_up, 0)
    lax.fori_loop(0, nch, start_down, 0)
    for load in loads:
        load.wait()

    npool, ns = pool.shape[:2]
    eye = lax.broadcasted_iota(jnp.int32, (ns, ns), 0) == lax.broadcasted_iota(
        jnp.int32, (ns, ns), 1
    )

    def column(ref, r):
        return jnp.sum(
            jnp.where(eye, jnp.broadcast_to(ref[r : r + 1, :], (ns, ns)), 0.0),
            axis=1,
            keepdims=True,
        )

    b_cols = [column(b_proj, r) for r in range(rows_dev)]
    c_cols = [column(c_proj, r) for r in range(rows_dev)]
    local = [slots[r] - e * npool for r in range(rows_dev)]
    block = 512 if chl % 512 == 0 else chl
    taps = conv_w.shape[0]

    def mixer(i, carry):
        cols = pl.ds(pl.multiple_of(i * block, block), block)
        rates = jnp.exp(a_log[:, cols])
        xin = conv_in[:, cols].astype(F32)
        step_all = step_in[:, cols].astype(F32) + step_b[:, cols]
        step_all = jnp.maximum(step_all, 0.0) + jnp.log1p(jnp.exp(-jnp.abs(step_all)))
        gate_all = jax.nn.silu(gate_in[:, cols].astype(F32))
        weights = conv_w[:, cols]
        bias = conv_b[:, cols]
        skip = d_skip[:, cols]
        outs = []
        for r in range(rows_dev):
            hist = cpool[0, :, cols].astype(F32)
            state = pool[0, :, cols].astype(F32)
            for q in range(1, npool):
                mine = local[r] == q
                hist = jnp.where(mine, cpool[q, :, cols].astype(F32), hist)
                state = jnp.where(mine, pool[q, :, cols].astype(F32), state)
            acc = weights[taps - 1 : taps] * xin[r : r + 1] + bias
            for lag in range(taps - 1):
                acc = acc + weights[lag : lag + 1] * hist[lag : lag + 1]
            conv = jax.nn.silu(acc)
            size = step_all[r : r + 1]
            nxt = jnp.exp(-(size * rates)) * state + (size * conv) * b_cols[r]
            nsbuf[r, :, cols] = nxt.astype(BF16)
            outs.append(jnp.sum(c_cols[r] * nxt, axis=0, keepdims=True) + skip * conv)
        gated = jnp.concatenate(outs, axis=0) * gate_all
        gsend[:, cols] = gated.astype(BF16)
        return carry

    lax.fori_loop(0, chl // block, mixer, 0)
    lane = lax.broadcasted_iota(jnp.int32, (rows_dev, LANES), 1)
    wide_probs = probs[...].astype(F32)
    coefs = jnp.zeros((rows_dev, LANES), F32)
    for k in range(ids.shape[1]):
        coefs = coefs + jnp.where(lane == ids[:, k : k + 1], wide_probs[:, k : k + 1], 0.0)
    gsend[:, chl:] = coefs.astype(BF16)

    pl.semaphore_wait(barrier, 2 * peers - 1)

    def gated_copy(dst, slot, p):
        return pltpu.make_async_remote_copy(
            src_ref=gsend,
            dst_ref=grecv.at[dst],
            send_sem=gs_sem.at[slot],
            recv_sem=gr_sem.at[dst],
            device_id={"expert": p, "tensor": t},
            device_id_type=MESH,
        )

    def resid_copy(dst, slot, p):
        return pltpu.make_async_remote_copy(
            src_ref=resid,
            dst_ref=rrecv.at[dst],
            send_sem=rs_sem.at[slot],
            recv_sem=rr_sem.at[dst],
            device_id={"expert": p, "tensor": t},
            device_id_type=MESH,
        )

    def mix_copy(dst, slot, p):
        return pltpu.make_async_remote_copy(
            src_ref=mix,
            dst_ref=mrecv.at[dst],
            send_sem=ms_sem.at[slot],
            recv_sem=mr_sem.at[dst],
            device_id={"expert": p, "tensor": t},
            device_id_type=MESH,
        )

    each_peer(lambda p: gated_copy(e, p, p).start())
    each_peer(lambda p: resid_copy(e, p, p).start())
    ns_store = pltpu.make_async_copy(nsbuf, ns_hbm, ns_sem)
    ns_store.start()
    grecv[e] = gsend[...]
    rrecv[e] = resid[...]
    outw_load.wait()
    each_peer(lambda p: gated_copy(p, p, p).wait_recv())
    for p in range(peers):
        gat[p * rows_dev : (p + 1) * rows_dev, :] = grecv[p].astype(F32)

    part[...] = jnp.dot(gat[:, :chl].astype(BF16), outw[...], preferred_element_type=F32)
    swap = pltpu.make_async_remote_copy(
        src_ref=part,
        dst_ref=part_in,
        send_sem=part_sem.at[0],
        recv_sem=part_sem.at[1],
        device_id={"expert": e, "tensor": other},
        device_id_type=MESH,
    )
    swap.start()
    swap.wait_recv()
    mix[...] = (part[...] + part_in[...]).astype(BF16)
    each_peer(lambda p: mix_copy(e, p, p).start())
    mrecv[e] = mix[...]
    each_peer(lambda p: resid_copy(p, p, p).wait_recv())
    for p in range(peers):
        hid[p * rows_dev : (p + 1) * rows_dev, :] = rrecv[p].astype(F32)
    each_peer(lambda p: mix_copy(p, p, p).wait_recv())
    total = jnp.zeros((rows, 1), F32)
    for p in range(peers):
        cols = slice(p * cb, (p + 1) * cb)
        wide = (hid[:, cols] + mrecv[p].astype(F32)).astype(BF16).astype(F32)
        hid[:, cols] = wide
        total = total + jnp.sum(wide * wide, axis=1, keepdims=True)
    scale = lax.rsqrt(total / d + 1e-05)
    normed[...] = (hid[...] * scale * gain[...]).astype(BF16)

    first_unit = (e * 2 + t) * units
    lower = first_unit // ff
    boundary = (lower + 1) * ff - first_unit
    all_coefs = gat[:, chl:]
    wide_lane = lax.broadcasted_iota(jnp.int32, (rows, LANES), 1)
    lower_coef = jnp.sum(jnp.where(wide_lane == lower, all_coefs, 0.0), axis=1, keepdims=True)
    upper_coef = jnp.sum(jnp.where(wide_lane == lower + 1, all_coefs, 0.0), axis=1, keepdims=True)

    def gate_up(c, carry):
        weight(0, c).wait()
        weight(1, c).wait()
        x = normed[...]
        g = lax.dot_general(x, gbuf[c], TRANS, preferred_element_type=F32)
        u = lax.dot_general(x, ubuf[c], TRANS, preferred_element_type=F32)
        h = jax.nn.silu(g) * u
        unit = c * ub + lax.broadcasted_iota(jnp.int32, (rows, ub), 1)
        h3[c, :rows, :] = jnp.where(unit < boundary, h, 0.0).astype(BF16)
        h3[c, rows:, :] = jnp.where(unit >= boundary, h, 0.0).astype(BF16)
        return carry

    lax.fori_loop(0, nch, gate_up, 0)
    lax.fori_loop(0, nch, lambda c, carry: (weight(2, c).wait(), carry)[1], 0)

    def out_copy(j, slot, src, p):
        return pltpu.make_async_remote_copy(
            src_ref=osend.at[j, slot],
            dst_ref=orecv.at[j % nj2, src],
            send_sem=os_sem.at[j, slot],
            recv_sem=or_sem.at[j % nj2, src],
            device_id={"expert": p, "tensor": j // nj2},
            device_id_type=MESH,
        )

    me = e * 2 + t
    for j in range(NJ):
        cols = slice(j * cw, (j + 1) * cw)

        def down(c, acc):
            return acc + jnp.dot(h3[c], dbuf[c, :, cols], preferred_element_type=F32)

        acc = lax.fori_loop(0, nch, down, jnp.zeros((2 * rows, cw), F32))
        comb = (lower_coef * acc[:rows] + upper_coef * acc[rows:]).astype(BF16).astype(F32)
        for p in range(peers):
            osend[j, p] = comb[p * rows_dev : (p + 1) * rows_dev].astype(BF16)
        each_peer(lambda p: out_copy(j, p, me, p).start())

        @pl.when(t != j // nj2)
        def _():
            out_copy(j, e, me, e).start()

    mine = pl.ds(pl.multiple_of(t * half, half), half)
    own = hid[:rows_dev, mine]
    for p in range(1, peers):
        own = jnp.where(e == p, hid[p * rows_dev : (p + 1) * rows_dev, mine], own)
    for jj in range(nj2):
        orecv[jj, me] = osend[t * nj2 + jj, e]
    for jj in range(nj2):
        each_peer(lambda p: out_copy(jj, p, p * 2, p).wait_recv())
        each_peer(lambda p: out_copy(jj, p, p * 2 + 1, p).wait_recv())
        out_copy(jj, e, e * 2 + other, e).wait_recv()
        cols = slice(jj * cw, (jj + 1) * cw)
        routed = jnp.sum(orecv[jj].astype(F32), axis=0)
        fin[t, :, cols] = (own[:, cols] + routed).astype(BF16)
    done = pltpu.make_async_remote_copy(
        src_ref=fin.at[t],
        dst_ref=fin.at[t],
        send_sem=fin_sem.at[0],
        recv_sem=fin_sem.at[1],
        device_id={"expert": e, "tensor": other},
        device_id_type=MESH,
    )
    done.start()
    each_peer(lambda p: gated_copy(e, p, p).wait_send())
    each_peer(lambda p: resid_copy(e, p, p).wait_send())
    each_peer(lambda p: mix_copy(e, p, p).wait_send())
    swap.wait_send()
    for j in range(NJ):
        each_peer(lambda p: out_copy(j, p, me, p).wait_send())

        @pl.when(t != j // nj2)
        def _():
            out_copy(j, e, me, e).wait_send()

    ns_store.wait()
    done.wait()
    out_ref[:, :half] = fin[0]
    out_ref[:, half:] = fin[1]


def local(
    peers,
    conv_input,
    gate_input,
    step_input,
    b_proj,
    c_proj,
    slot_ids,
    state_pool,
    conv_pool,
    conv_weight,
    conv_bias,
    step_bias,
    a_log,
    d_skip,
    out_weight,
    residual,
    norm_gain,
    expert_ids,
    expert_probs,
    gate_weight,
    up_weight,
    down_weight,
):
    rows_dev, chl = conv_input.shape
    d = residual.shape[1]
    rows = rows_dev * peers
    units = gate_weight.shape[0]
    ub = unit_block(units)
    nch = units // ub
    cb = out_weight.shape[1]
    ns = state_pool.shape[1]
    cw = d // NJ
    small = (
        conv_input,
        gate_input,
        step_input,
        b_proj,
        c_proj,
        state_pool,
        conv_pool,
        conv_weight,
        conv_bias[None],
        step_bias[None],
        a_log,
        d_skip[None],
        residual,
        norm_gain[None],
        expert_ids,
        expert_probs,
    )
    sem = pltpu.SemaphoreType.DMA
    weights = pltpu.VMEM((nch, ub, d), BF16)
    hbm = pl.BlockSpec(memory_space=pl.ANY)
    return pl.pallas_call(
        functools.partial(kernel, peers),
        out_shape=(
            jax.ShapeDtypeStruct((rows_dev, d), BF16),
            jax.ShapeDtypeStruct((rows_dev, ns, chl), BF16),
        ),
        in_specs=[pl.BlockSpec(memory_space=pltpu.SMEM)] + [hbm] * (SMALL + 4),
        out_specs=(pl.BlockSpec(memory_space=pltpu.VMEM), hbm),
        scratch_shapes=[pltpu.VMEM(x.shape, x.dtype) for x in small]
        + [
            sem((SMALL,)),
            pltpu.VMEM((chl, cb), BF16),
            sem(()),
            weights,
            weights,
            weights,
            sem((3, nch)),
            pltpu.VMEM((rows_dev, chl + LANES), BF16),
            pltpu.VMEM((peers, rows_dev, chl + LANES), BF16),
            sem((peers,)),
            sem((peers,)),
            pltpu.VMEM((peers, rows_dev, d), BF16),
            sem((peers,)),
            sem((peers,)),
            pltpu.VMEM((rows, chl + LANES), F32),
            pltpu.VMEM((rows, cb), F32),
            pltpu.VMEM((rows, cb), F32),
            sem((2,)),
            pltpu.VMEM((rows, cb), BF16),
            pltpu.VMEM((peers, rows, cb), BF16),
            sem((peers,)),
            sem((peers,)),
            pltpu.VMEM((rows, d), F32),
            pltpu.VMEM((rows, d), BF16),
            pltpu.VMEM((nch, 2 * rows, ub), BF16),
            pltpu.VMEM((NJ, peers, rows_dev, cw), BF16),
            pltpu.VMEM((NJ // 2, 2 * peers, rows_dev, cw), BF16),
            sem((NJ, peers)),
            sem((NJ // 2, 2 * peers)),
            pltpu.VMEM((2, rows_dev, d // 2), BF16),
            sem((2,)),
            pltpu.VMEM((rows_dev, ns, chl), BF16),
            sem(()),
        ],
        compiler_params=pltpu.CompilerParams(
            collective_id=0, has_side_effects=True, vmem_limit_bytes=67043328
        ),
    )(slot_ids, *small, out_weight, gate_weight, up_weight, down_weight)


def solution(mesh):
    return jax.shard_map(
        functools.partial(local, mesh.shape["expert"]),
        mesh=mesh,
        in_specs=(
            P(("groups", "expert"), "tensor"),
            P(("groups", "expert"), "tensor"),
            P(("groups", "expert"), "tensor"),
            P(("groups", "expert"), None),
            P(("groups", "expert"), None),
            P(("groups", "expert")),
            P(("groups", "expert"), None, "tensor"),
            P(("groups", "expert"), None, "tensor"),
            P(None, "tensor"),
            P("tensor"),
            P("tensor"),
            P(None, "tensor"),
            P("tensor"),
            P("tensor", "expert"),
            P(("groups", "expert"), None),
            P(),
            P(("groups", "expert"), None),
            P(("groups", "expert"), None),
            P(("expert", "tensor"), None),
            P(("expert", "tensor"), None),
            P(("expert", "tensor"), None),
        ),
        out_specs=(P(("groups", "expert"), None), P(("groups", "expert"), None, "tensor")),
        check_vma=False,
    )
```

```python
import functools

import jax
import jax.numpy as jnp
from jax import lax
from jax.experimental import pallas as pl
from jax.experimental.pallas import tpu as pltpu
from jax.sharding import PartitionSpec as P

EXPERTS = 3
LANES = 128
F32 = jnp.float32
BF16 = jnp.bfloat16
TRANS = (((1,), (1,)), ((), ()))
MESH = pl.DeviceIdType.MESH
NJ = 4
SMALL = 16


def unit_block(units):
    for block in (256, 384, 128):
        if units % block == 0:
            return block
    return units


def kernel(
    peers,
    slots,
    *refs,
):
    small_hbm = refs[:SMALL]
    outw_hbm, gate_hbm, up_hbm, down_hbm = refs[SMALL : SMALL + 4]
    out_ref, ns_hbm = refs[SMALL + 4 : SMALL + 6]
    small = refs[SMALL + 6 : 2 * SMALL + 6]
    (
        small_sem,
        outw,
        outw_sem,
        gbuf,
        ubuf,
        dbuf,
        w_sem,
        gsend,
        grecv,
        gs_sem,
        gr_sem,
        rrecv,
        rs_sem,
        rr_sem,
        gat,
        part,
        part_in,
        part_sem,
        mix,
        mrecv,
        ms_sem,
        mr_sem,
        hid,
        gacc,
        uacc,
        h2,
        osend,
        orecv,
        os_sem,
        or_sem,
        fin,
        fin_sem,
        nsbuf,
        ns_sem,
    ) = refs[2 * SMALL + 6 :]
    (
        conv_in,
        gate_in,
        step_in,
        b_proj,
        c_proj,
        pool,
        cpool,
        conv_w,
        conv_b,
        step_b,
        a_log,
        d_skip,
        resid,
        gain,
        ids,
        probs,
    ) = small
    e = lax.axis_index("expert")
    t = lax.axis_index("tensor")
    other = 1 - t
    nch, ub, d = gbuf.shape
    rows_dev, chl = conv_in.shape
    rows = rows_dev * peers
    units = nch * ub
    ff = units * peers * 2 // EXPERTS
    cb = outw.shape[1]
    half = d // 2
    nj2 = NJ // 2
    cw = d // NJ

    def peer(k):
        return lax.rem(e + k, peers)

    def each_peer(body):
        def step(k, carry):
            body(peer(k))
            return carry

        lax.fori_loop(1, peers, step, 0)

    barrier = pltpu.get_barrier_semaphore()
    pl.semaphore_signal(
        barrier, inc=1, device_id={"expert": e, "tensor": other}, device_id_type=MESH
    )

    def greet(p):
        pl.semaphore_signal(barrier, inc=1, device_id={"expert": p, "tensor": t}, device_id_type=MESH)
        pl.semaphore_signal(
            barrier, inc=1, device_id={"expert": p, "tensor": other}, device_id_type=MESH
        )

    each_peer(greet)

    loads = [
        pltpu.make_async_copy(src, dst, small_sem.at[i])
        for i, (src, dst) in enumerate(zip(small_hbm, small))
    ]
    for load in loads:
        load.start()
    outw_load = pltpu.make_async_copy(outw_hbm, outw, outw_sem)
    outw_load.start()

    def weight(which, c):
        src = (gate_hbm, up_hbm, down_hbm)[which]
        span = pl.ds(pl.multiple_of(c * ub, ub), ub)
        dst = (gbuf, ubuf)[which].at[c] if which < 2 else dbuf.at[span]
        return pltpu.make_async_copy(src.at[span], dst, w_sem.at[which, c])

    def start_gate_up(c, carry):
        weight(0, c).start()
        weight(1, c).start()
        return carry

    def start_down(c, carry):
        weight(2, c).start()
        return carry

    lax.fori_loop(0, nch, start_gate_up, 0)
    lax.fori_loop(0, nch, start_down, 0)
    for load in loads:
        load.wait()

    npool, ns = pool.shape[:2]
    eye = lax.broadcasted_iota(jnp.int32, (ns, ns), 0) == lax.broadcasted_iota(
        jnp.int32, (ns, ns), 1
    )

    def column(ref, r):
        return jnp.sum(
            jnp.where(eye, jnp.broadcast_to(ref[r : r + 1, :], (ns, ns)), 0.0),
            axis=1,
            keepdims=True,
        )

    b_cols = [column(b_proj, r) for r in range(rows_dev)]
    c_cols = [column(c_proj, r) for r in range(rows_dev)]
    local = [slots[r] - e * npool for r in range(rows_dev)]
    block = 512 if chl % 512 == 0 else chl
    taps = conv_w.shape[0]

    def mixer(i, carry):
        cols = pl.ds(pl.multiple_of(i * block, block), block)
        rates = jnp.exp(a_log[:, cols])
        xin = conv_in[:, cols].astype(F32)
        step_all = step_in[:, cols].astype(F32) + step_b[:, cols]
        step_all = jnp.maximum(step_all, 0.0) + jnp.log1p(jnp.exp(-jnp.abs(step_all)))
        gate_all = jax.nn.silu(gate_in[:, cols].astype(F32))
        weights = conv_w[:, cols]
        bias = conv_b[:, cols]
        skip = d_skip[:, cols]
        outs = []
        for r in range(rows_dev):
            hist = cpool[:, 0, cols].astype(F32)
            state = pool[0, :, cols].astype(F32)
            for q in range(1, npool):
                mine = local[r] == q
                hist = jnp.where(mine, cpool[:, q, cols].astype(F32), hist)
                state = jnp.where(mine, pool[q, :, cols].astype(F32), state)
            acc = weights[taps - 1 : taps] * xin[r : r + 1] + bias
            for lag in range(taps - 1):
                acc = acc + weights[lag : lag + 1] * hist[lag : lag + 1]
            conv = jax.nn.silu(acc)
            size = step_all[r : r + 1]
            nxt = jnp.exp(-(size * rates)) * state + (size * conv) * b_cols[r]
            nsbuf[r, :, cols] = nxt.astype(BF16)
            outs.append(jnp.sum(c_cols[r] * nxt, axis=0, keepdims=True) + skip * conv)
        gated = jnp.concatenate(outs, axis=0) * gate_all
        gsend[:, cols] = gated.astype(BF16)
        return carry

    lax.fori_loop(0, chl // block, mixer, 0)
    lane = lax.broadcasted_iota(jnp.int32, (rows_dev, LANES), 1)
    wide_probs = probs[...].astype(F32)
    coefs = jnp.zeros((rows_dev, LANES), F32)
    for k in range(ids.shape[1]):
        coefs = coefs + jnp.where(lane == ids[:, k : k + 1], wide_probs[:, k : k + 1], 0.0)
    gsend[:, chl:] = coefs.astype(BF16)

    pl.semaphore_wait(barrier, 2 * peers - 1)

    def gated_copy(dst, slot, p):
        return pltpu.make_async_remote_copy(
            src_ref=gsend,
            dst_ref=grecv.at[dst],
            send_sem=gs_sem.at[slot],
            recv_sem=gr_sem.at[dst],
            device_id={"expert": p, "tensor": t},
            device_id_type=MESH,
        )

    def resid_copy(dst, slot, p):
        return pltpu.make_async_remote_copy(
            src_ref=resid,
            dst_ref=rrecv.at[dst],
            send_sem=rs_sem.at[slot],
            recv_sem=rr_sem.at[dst],
            device_id={"expert": p, "tensor": t},
            device_id_type=MESH,
        )

    def mix_copy(dst, slot, p):
        return pltpu.make_async_remote_copy(
            src_ref=mix,
            dst_ref=mrecv.at[dst],
            send_sem=ms_sem.at[slot],
            recv_sem=mr_sem.at[dst],
            device_id={"expert": p, "tensor": t},
            device_id_type=MESH,
        )

    each_peer(lambda p: gated_copy(e, p, p).start())
    each_peer(lambda p: resid_copy(e, p, p).start())
    ns_store = pltpu.make_async_copy(nsbuf, ns_hbm, ns_sem)
    ns_store.start()
    grecv[e] = gsend[...]
    rrecv[e] = resid[...]
    outw_load.wait()
    each_peer(lambda p: gated_copy(p, p, p).wait_recv())
    for p in range(peers):
        gat[p * rows_dev : (p + 1) * rows_dev, :] = grecv[p].astype(F32)

    part[...] = jnp.dot(gat[:, :chl].astype(BF16), outw[...], preferred_element_type=F32)
    swap = pltpu.make_async_remote_copy(
        src_ref=part,
        dst_ref=part_in,
        send_sem=part_sem.at[0],
        recv_sem=part_sem.at[1],
        device_id={"expert": e, "tensor": other},
        device_id_type=MESH,
    )
    swap.start()
    swap.wait_recv()
    mix[...] = (part[...] + part_in[...]).astype(BF16)
    each_peer(lambda p: mix_copy(e, p, p).start())
    mrecv[e] = mix[...]
    each_peer(lambda p: resid_copy(p, p, p).wait_recv())
    for p in range(peers):
        hid[p * rows_dev : (p + 1) * rows_dev, :] = rrecv[p].astype(F32)
    def wait_gate_up(c, carry):
        weight(0, c).wait()
        weight(1, c).wait()
        return carry

    def products(x, cols, first):
        for c in range(nch):
            g = lax.dot_general(x, gbuf[c, :, cols], TRANS, preferred_element_type=F32)
            u = lax.dot_general(x, ubuf[c, :, cols], TRANS, preferred_element_type=F32)
            gacc[c] = g if first else gacc[c] + g
            uacc[c] = u if first else uacc[c] + u

    def arrived(p, cols):
        wide = (hid[:, cols] + mrecv[p].astype(F32)).astype(BF16).astype(F32)
        hid[:, cols] = wide
        return wide

    def squares(wide):
        return jnp.sum(wide * wide, axis=1, keepdims=True)

    lax.fori_loop(0, nch, wait_gate_up, 0)
    if cb % LANES == 0 and peers % 2 == 0:

        def nearest(k):
            far = e // (peers // 2)
            edge = e * (1 - far) + (peers - 1 - e) * far
            inside = (2 * edge - k + 2 * peers) // (2 * peers)
            step = (k + 1) // 2
            odd = k % 2
            paired = e + step * (2 * odd - 1)
            single = k * (1 - far) + (peers - 1 - k) * far
            return inside * paired + (1 - inside) * single

        def columns_of(p):
            return pl.ds(pl.multiple_of(p * cb, cb), cb)

        cols = columns_of(e)
        wide = arrived(e, cols)
        products((wide * gain[:, cols]).astype(BF16), cols, True)

        def next_block(k, total):
            p = nearest(k)
            mix_copy(p, p, p).wait_recv()
            cols = columns_of(p)
            wide = arrived(p, cols)
            products((wide * gain[:, cols]).astype(BF16), cols, False)
            return total + squares(wide)

        total = lax.fori_loop(1, peers, next_block, squares(wide))
    else:
        each_peer(lambda p: mix_copy(p, p, p).wait_recv())
        total = jnp.zeros((rows, 1), F32)
        for p in range(peers):
            total = total + squares(arrived(p, slice(p * cb, (p + 1) * cb)))
        products((hid[...] * gain[...]).astype(BF16), slice(0, d), True)
    scale = lax.rsqrt(total / d + 1e-05)

    first_unit = (e * 2 + t) * units
    lower = first_unit // ff
    boundary = (lower + 1) * ff - first_unit
    all_coefs = gat[:, chl:]
    wide_lane = lax.broadcasted_iota(jnp.int32, (rows, LANES), 1)
    lower_coef = jnp.sum(jnp.where(wide_lane == lower, all_coefs, 0.0), axis=1, keepdims=True)
    upper_coef = jnp.sum(jnp.where(wide_lane == lower + 1, all_coefs, 0.0), axis=1, keepdims=True)

    for c in range(nch):
        h = jax.nn.silu(gacc[c] * scale) * (uacc[c] * scale)
        unit = c * ub + lax.broadcasted_iota(jnp.int32, (rows, ub), 1)
        here = slice(c * ub, (c + 1) * ub)
        h2[:rows, here] = jnp.where(unit < boundary, h, 0.0).astype(BF16)
        h2[rows:, here] = jnp.where(unit >= boundary, h, 0.0).astype(BF16)
    lax.fori_loop(0, nch, lambda c, carry: (weight(2, c).wait(), carry)[1], 0)

    def out_copy(j, slot, src, p):
        return pltpu.make_async_remote_copy(
            src_ref=osend.at[j, slot],
            dst_ref=orecv.at[j % nj2, src],
            send_sem=os_sem.at[j, slot],
            recv_sem=or_sem.at[j % nj2, src],
            device_id={"expert": p, "tensor": j // nj2},
            device_id_type=MESH,
        )

    me = e * 2 + t
    for j in range(NJ):
        cols = slice(j * cw, (j + 1) * cw)
        acc = jnp.dot(h2[...], dbuf[:, cols], preferred_element_type=F32)
        comb = (lower_coef * acc[:rows] + upper_coef * acc[rows:]).astype(BF16).astype(F32)
        for p in range(peers):
            osend[j, p] = comb[p * rows_dev : (p + 1) * rows_dev].astype(BF16)
        each_peer(lambda p: out_copy(j, p, me, p).start())

        @pl.when(t != j // nj2)
        def _():
            out_copy(j, e, me, e).start()

    mine = pl.ds(pl.multiple_of(t * half, half), half)
    own = hid[:rows_dev, mine]
    for p in range(1, peers):
        own = jnp.where(e == p, hid[p * rows_dev : (p + 1) * rows_dev, mine], own)
    for jj in range(nj2):
        orecv[jj, me] = osend[t * nj2 + jj, e]
    for jj in range(nj2):
        each_peer(lambda p: out_copy(jj, p, p * 2, p).wait_recv())
        each_peer(lambda p: out_copy(jj, p, p * 2 + 1, p).wait_recv())
        out_copy(jj, e, e * 2 + other, e).wait_recv()
        cols = slice(jj * cw, (jj + 1) * cw)
        routed = jnp.sum(orecv[jj].astype(F32), axis=0)
        fin[t, :, cols] = (own[:, cols] + routed).astype(BF16)
    done = pltpu.make_async_remote_copy(
        src_ref=fin.at[t],
        dst_ref=fin.at[t],
        send_sem=fin_sem.at[0],
        recv_sem=fin_sem.at[1],
        device_id={"expert": e, "tensor": other},
        device_id_type=MESH,
    )
    done.start()
    each_peer(lambda p: gated_copy(e, p, p).wait_send())
    each_peer(lambda p: resid_copy(e, p, p).wait_send())
    each_peer(lambda p: mix_copy(e, p, p).wait_send())
    swap.wait_send()
    for j in range(NJ):
        each_peer(lambda p: out_copy(j, p, me, p).wait_send())

        @pl.when(t != j // nj2)
        def _():
            out_copy(j, e, me, e).wait_send()

    ns_store.wait()
    done.wait()
    out_ref[:, :half] = fin[0]
    out_ref[:, half:] = fin[1]


def local(
    peers,
    conv_input,
    gate_input,
    step_input,
    b_proj,
    c_proj,
    slot_ids,
    state_pool,
    conv_pool,
    conv_weight,
    conv_bias,
    step_bias,
    a_log,
    d_skip,
    out_weight,
    residual,
    norm_gain,
    expert_ids,
    expert_probs,
    gate_weight,
    up_weight,
    down_weight,
):
    rows_dev, chl = conv_input.shape
    d = residual.shape[1]
    rows = rows_dev * peers
    units = gate_weight.shape[0]
    ub = unit_block(units)
    nch = units // ub
    cb = out_weight.shape[1]
    ns = state_pool.shape[1]
    cw = d // NJ
    small = (
        conv_input,
        gate_input,
        step_input,
        b_proj,
        c_proj,
        state_pool,
        conv_pool.transpose(1, 0, 2),
        conv_weight,
        conv_bias[None],
        step_bias[None],
        a_log,
        d_skip[None],
        residual,
        norm_gain[None],
        expert_ids,
        expert_probs,
    )
    sem = pltpu.SemaphoreType.DMA
    weights = pltpu.VMEM((nch, ub, d), BF16)
    hbm = pl.BlockSpec(memory_space=pl.ANY)
    return pl.pallas_call(
        functools.partial(kernel, peers),
        out_shape=(
            jax.ShapeDtypeStruct((rows_dev, d), BF16),
            jax.ShapeDtypeStruct((rows_dev, ns, chl), BF16),
        ),
        in_specs=[pl.BlockSpec(memory_space=pltpu.SMEM)] + [hbm] * (SMALL + 4),
        out_specs=(pl.BlockSpec(memory_space=pltpu.VMEM), hbm),
        scratch_shapes=[pltpu.VMEM(x.shape, x.dtype) for x in small]
        + [
            sem((SMALL,)),
            pltpu.VMEM((chl, cb), BF16),
            sem(()),
            weights,
            weights,
            pltpu.VMEM((units, d), BF16),
            sem((3, nch)),
            pltpu.VMEM((rows_dev, chl + LANES), BF16),
            pltpu.VMEM((peers, rows_dev, chl + LANES), BF16),
            sem((peers,)),
            sem((peers,)),
            pltpu.VMEM((peers, rows_dev, d), BF16),
            sem((peers,)),
            sem((peers,)),
            pltpu.VMEM((rows, chl + LANES), F32),
            pltpu.VMEM((rows, cb), F32),
            pltpu.VMEM((rows, cb), F32),
            sem((2,)),
            pltpu.VMEM((rows, cb), BF16),
            pltpu.VMEM((peers, rows, cb), BF16),
            sem((peers,)),
            sem((peers,)),
            pltpu.VMEM((rows, d), F32),
            pltpu.VMEM((nch, rows, ub), F32),
            pltpu.VMEM((nch, rows, ub), F32),
            pltpu.VMEM((2 * rows, units), BF16),
            pltpu.VMEM((NJ, peers, rows_dev, cw), BF16),
            pltpu.VMEM((NJ // 2, 2 * peers, rows_dev, cw), BF16),
            sem((NJ, peers)),
            sem((NJ // 2, 2 * peers)),
            pltpu.VMEM((2, rows_dev, d // 2), BF16),
            sem((2,)),
            pltpu.VMEM((rows_dev, ns, chl), BF16),
            sem(()),
        ],
        compiler_params=pltpu.CompilerParams(
            collective_id=0, has_side_effects=True, vmem_limit_bytes=67043328
        ),
    )(slot_ids, *small, out_weight, gate_weight, up_weight, down_weight)


def solution(mesh):
    return jax.shard_map(
        functools.partial(local, mesh.shape["expert"]),
        mesh=mesh,
        in_specs=(
            P(("groups", "expert"), "tensor"),
            P(("groups", "expert"), "tensor"),
            P(("groups", "expert"), "tensor"),
            P(("groups", "expert"), None),
            P(("groups", "expert"), None),
            P(("groups", "expert")),
            P(("groups", "expert"), None, "tensor"),
            P(("groups", "expert"), None, "tensor"),
            P(None, "tensor"),
            P("tensor"),
            P("tensor"),
            P(None, "tensor"),
            P("tensor"),
            P("tensor", "expert"),
            P(("groups", "expert"), None),
            P(),
            P(("groups", "expert"), None),
            P(("groups", "expert"), None),
            P(("expert", "tensor"), None),
            P(("expert", "tensor"), None),
            P(("expert", "tensor"), None),
        ),
        out_specs=(P(("groups", "expert"), None), P(("groups", "expert"), None, "tensor")),
        check_vma=False,
    )
```
